32 devices in a mesh: ka: 8 (over z, x), pt: 4 (over y, core).
Axes of the slice: x: 2, y: 2, z: 4, core: 2. Of those that a mesh axis runs over, the one named last changes fastest.
Arguments:
- wedge_orbitals: bfloat16 [2, 8, 4096, 128], P(None, 'ka', 'pt'), may hold values from -6 to 6
- star_members: int32 [8, 4], replicated, may hold values from -1 to 7, as said below
- star_ops: int32 [8, 4], replicated, may hold values from 0 to 47
- rotations: bfloat16 [48, 128, 128], replicated, may hold values from -0.5 to 0.5
- screen_left: bfloat16 [6, 4096, 64], P(None, 'pt'), may hold values from -2.5 to 2.5
- screen_right: bfloat16 [6, 4096, 64], P(None, 'pt'), may hold values from -2.5 to 2.5
Outputs:
- exchange_matrix: float32 [2, 8, 128, 128], P(None, 'ka', 'pt')
The draws below stay inside these ranges and needn't reach their ends.
Inputs may be any that keep to these rules, and one draw needn't show every extreme that they name: `star_members`: every k-point 0 to 7 stands exactly once in the table; -1 marks an empty slot; the star of some wedge point fills all 4 slots.
All inputs are finite; a program needn't handle non-finite values.
Results may differ from the reference program's by a relative error of at most 0.0064.
Values may be sent and summed in bfloat16 or wider, within the bound.
No kernel may reach another device: no remote copies, remote signals or barrier semaphores. Data moves between devices by JAX's collectives and lax.ppermute only.
A program may use at most 128 MiB of HBM per device.

```python
import math
import jax
import jax.numpy as jnp
from jax import lax

NB = 128
NPTS = 4096
RANK = 64
NOPS = 48
MULT = 4
STOPS = 6
QBLK = 1024
NK = 8
NW = 8


def draw_star_members(key, part):
    n_slots = NW * MULT
    key_row = jax.random.fold_in(key, 11)
    key_slots = jax.random.fold_in(key, 12)
    key_kpts = jax.random.fold_in(key, 13)
    full_row = jax.random.randint(key_row, (), 0, NW)
    slot_order = jax.random.permutation(key_slots, n_slots).astype(jnp.int32)
    row_of = slot_order // MULT
    scores = jnp.where(row_of == full_row, 0, 1).astype(jnp.int32) * n_slots + jnp.arange(n_slots, dtype=jnp.int32)
    ranking = jnp.argsort(scores, stable=True)
    chosen = slot_order[ranking][:NK]
    kpoint_order = jax.random.permutation(key_kpts, NK).astype(jnp.int32)
    table = jnp.full((n_slots,), -1, jnp.int32).at[chosen].set(kpoint_order)
    return table.reshape(NW, MULT)


def set_ends(values, rng, low, high):
    place = [jax.random.randint(jax.random.fold_in(rng, axis), (), 0, length) for axis, length in enumerate(values.shape)]
    main_axis = values.shape.index(max(values.shape))
    next_to = place[:main_axis] + [(place[main_axis] + 1) % values.shape[main_axis]] + place[main_axis + 1:]
    return values.at[tuple(place)].set(low).at[tuple(next_to)].set(high)


def steps_of(own_key, shape, split, least, high):
    factor_of = 1.0
    for dim, parts in split:
        steps = jax.random.uniform(jax.random.fold_in(jax.random.fold_in(own_key, 6), dim), (parts,), jnp.float32, least / len(split), high / len(split))
        factor_of = factor_of * jnp.repeat(jnp.exp(steps), shape[dim] // parts).reshape((-1,) + (1,) * (len(shape) - 1 - dim))
    return factor_of


def noise(rng, shape, deviation, limit, pieces=(), kind=jnp.bfloat16):
    gain = steps_of(rng, shape, pieces, -0.22, 0.18) if pieces else 1.0
    result = jax.random.normal(rng, shape, jnp.float32) * deviation * gain
    return jnp.minimum(jnp.maximum(result, -limit), limit).astype(kind)


def setup_inputs(seed: int = 0) -> dict:
    splits = jax.random.split(jax.random.key(seed), 7)
    return {
        "wedge_orbitals": noise(splits[0], (2, NW, NPTS, NB), 1.0, 6.0, ((1, 8), (2, 4))),
        "star_members": draw_star_members(jax.random.fold_in(splits[6], 71), 0),
        "star_ops": set_ends(jax.random.randint(splits[2], (NW, MULT), 0, NOPS), jax.random.fold_in(splits[2], 1), 0, NOPS - 1).astype(jnp.int32),
        "rotations": noise(splits[3], (NOPS, NB, NB), NB ** -0.5, 0.5),
        "screen_left": noise(splits[4], (STOPS, NPTS, RANK), 0.35, 2.5, ((1, 4),)),
        "screen_right": noise(splits[5], (STOPS, NPTS, RANK), 0.35, 2.5, ((1, 4),)),
    }


def rotated_blocks(wedge_orbitals, star_members, star_ops, rotations):
    wedge_iota = jnp.arange(NW, dtype=jnp.int32)[:, None]

    def per_kpoint(kpoint):
        located = star_members == kpoint
        wedge_index = jnp.sum(jnp.where(located, wedge_iota, 0)).astype(jnp.int32)
        op_index = jnp.sum(jnp.where(located, star_ops, 0)).astype(jnp.int32)
        arrived = lax.dynamic_index_in_dim(wedge_orbitals, wedge_index, 1, keepdims=False)
        rotation = lax.dynamic_index_in_dim(rotations, op_index, 0, keepdims=False)
        product = jnp.dot(arrived.reshape(2 * NPTS, NB), rotation, preferred_element_type=jnp.float32)
        return product.astype(jnp.bfloat16).reshape(2, NPTS, NB)
    return lax.map(per_kpoint, jnp.arange(NK, dtype=jnp.int32))

def density_term(row_block, full_block, upper_half, lower_half, left_screen, right_screen):
    n_rows = row_block.shape[1]
    left_rows = jnp.concatenate([row_block[0], row_block[1]], axis=1)
    swapped = jnp.concatenate([row_block[1], -row_block[0]], axis=1)
    stacked = jnp.concatenate([left_rows, swapped], axis=0)
    accum = jnp.zeros((n_rows, 2 * NB), jnp.float32)
    for column_block in range(NPTS // QBLK):
        col_start = column_block * QBLK
        col_end = col_start + QBLK
        column_rows = jnp.concatenate([full_block[0, col_start:col_end], full_block[1, col_start:col_end]], axis=1)
        density = lax.dot_general(stacked, column_rows, (((1,), (1,)), ((), ())), preferred_element_type=jnp.float32)
        screen_tile = lax.dot_general(left_screen, right_screen[col_start:col_end], (((1,), (1,)), ((), ())), preferred_element_type=jnp.float32)
        real_part = (density[:n_rows] * screen_tile).astype(jnp.bfloat16)
        imag_part = (density[n_rows:] * screen_tile).astype(jnp.bfloat16)
        screened = jnp.concatenate([real_part, imag_part], axis=1)
        operand = jnp.concatenate([upper_half[col_start:col_end], lower_half[col_start:col_end]], axis=0)
        accum = accum + jnp.dot(screened, operand, preferred_element_type=jnp.float32)
    return accum

def reference(wedge_orbitals, star_members, star_ops, rotations, screen_left, screen_right):
    blocks = rotated_blocks(wedge_orbitals, star_members, star_ops, rotations)
    lead_stops = STOPS // 2
    scale_factor = 1.0 / (4.0 * NPTS * math.sqrt(NB))

    def per_kpoint(kpoint):
        own_block = lax.dynamic_index_in_dim(blocks, kpoint, 0, keepdims=False)
        upper_half = jnp.concatenate([own_block[0], own_block[1]], axis=1)
        lower_half = jnp.concatenate([-own_block[1], own_block[0]], axis=1)
        accum = jnp.zeros((NPTS, 2 * NB), jnp.float32)
        for stop in range(STOPS):
            other = ((kpoint + lead_stops - stop) % NK).astype(jnp.int32)
            visited = lax.dynamic_index_in_dim(blocks, other, 0, keepdims=False)
            accum = accum + density_term(visited, visited, upper_half, lower_half, screen_left[stop], screen_right[stop])
        rounded_y = accum.astype(jnp.bfloat16)
        y_real = rounded_y[:, :NB]
        y_imag = rounded_y[:, NB:]
        stacked_x = jnp.concatenate([own_block[0], own_block[1]], axis=0)
        right_stack = jnp.concatenate([rounded_y, jnp.concatenate([y_imag, -y_real], axis=1)], axis=0)
        partial_value = lax.dot_general(stacked_x, right_stack, (((0,), (0,)), ((), ())), preferred_element_type=jnp.float32)
        partial_value = partial_value * scale_factor
        return jnp.stack([partial_value[:, :NB], partial_value[:, NB:]])
    matrices = lax.map(per_kpoint, jnp.arange(NK, dtype=jnp.int32))
    return jnp.transpose(matrices, (1, 0, 2, 3))
```

```python
import functools
import math

import jax
import jax.numpy as jnp
from jax import lax
from jax.experimental import pallas as pl
from jax.experimental.pallas import tpu as pltpu
from jax.sharding import PartitionSpec as P

BF = jnp.bfloat16
F32 = jnp.float32


def swap_bit(array, axes, n_ka, n_pt, axis, bit):
    route = []
    for ka in range(n_ka):
        for pt in range(n_pt):
            other = (ka ^ bit, pt) if axis == "ka" else (ka, pt ^ bit)
            route.append((ka * n_pt + pt, other[0] * n_pt + other[1]))
    return lax.ppermute(array, axes, route)


def dot_last(a, b):
    return lax.dot_general(a, b, (((1,), (1,)), ((), ())), preferred_element_type=F32)


def dot_first(a, b):
    return lax.dot_general(a, b, (((0,), (0,)), ((), ())), preferred_element_type=F32)


def exchange_kernel(n_k, n_p, n_q, n_stops, blk, tile, n_out, scale, slot_ref, rot_ref, left_ref, right_ref, *refs):
    p_refs = refs[:n_p]
    q_refs = refs[n_p : n_p + n_q]
    out_ref = refs[n_p + n_q]
    op, ops, oq, oql, den_re, den_im, scr, wgt, acc = refs[n_p + n_q + 1 :]
    rows_p = n_p * blk
    rows_q = n_q * blk
    nb = op.shape[2] // 2
    lead = n_stops // 2

    def rotate(k, carry):
        slot = slot_ref[k]
        parts = []
        for ref in p_refs + q_refs:
            piece = ref[slot]
            parts.append(jnp.concatenate([piece[0], piece[1]], axis=1))
        stacked = jnp.concatenate(parts, axis=0)
        turned = jnp.dot(stacked, rot_ref[k], preferred_element_type=F32).astype(BF)
        first = turned[:rows_p]
        second = turned[rows_p:]
        op[k] = first
        ops[k] = jnp.concatenate([first[:, nb:], -first[:, :nb]], axis=1)
        oq[k] = second
        oql[k] = jnp.concatenate([-second[:, nb:], second[:, :nb]], axis=1)
        return carry

    lax.fori_loop(0, n_k, rotate, 0)

    for t in range(rows_q // tile):
        cols = pl.ds(t * tile, tile)

        def densities(j, carry):
            right = oq[j, cols, :]
            den_re[j] = dot_last(op[j], right)
            den_im[j] = dot_last(ops[j], right)
            return carry

        lax.fori_loop(0, n_k, densities, 0)
        for s in range(n_stops):
            scr[s] = dot_last(left_ref[s], right_ref[s, cols, :])

        def weigh(i, carry):
            rows = pl.ds(pl.multiple_of(i * 16, 16), 16)
            for half in range(tile // 128):
                lanes = pl.ds(half * 128, 128)
                screens = [scr[s, rows, lanes] for s in range(n_stops)]
                for part, den in ((0, den_re), (1, den_im)):
                    dens = [den[j, rows, lanes] for j in range(n_k)]
                    for k in range(n_k):
                        total = dens[(k + lead) % n_k] * screens[0]
                        for s in range(1, n_stops):
                            total = total + dens[(k + lead - s) % n_k] * screens[s]
                        wgt[k, rows, pl.ds(part * tile + half * 128, 128)] = total.astype(BF)
            return carry

        lax.fori_loop(0, rows_p // 16, weigh, 0)

        def apply(k, carry):
            weights = jnp.concatenate([oq[k, cols, :], oql[k, cols, :]], axis=0)
            product = jnp.dot(wgt[k], weights, preferred_element_type=F32)
            acc[k] = product if t == 0 else acc[k] + product
            return carry

        lax.fori_loop(0, n_k, apply, 0)

    def project(k, carry):
        gram = dot_first(op[k], acc[k].astype(BF)) * scale
        real = (gram[:nb, :nb] + gram[nb:, nb:]).astype(BF)
        imag = (gram[:nb, nb:] - gram[nb:, :nb]).astype(BF)
        step = nb // n_out
        for o in range(n_out):
            out_ref[k, o, 0] = real[o * step : (o + 1) * step]
            out_ref[k, o, 1] = imag[o * step : (o + 1) * step]
        return carry

    lax.fori_loop(0, n_k, project, 0)


def block_matrices(slots, rot2, left_rows, right_rows, p_blocks, q_blocks, n_out, scale):
    n_k = rot2.shape[0]
    blk, nb = p_blocks[0].shape[2:]
    n_stops = left_rows.shape[0]
    rows_p = len(p_blocks) * blk
    rows_q = len(q_blocks) * blk
    tile = min(256, rows_q)
    vmem = pl.BlockSpec(memory_space=pltpu.VMEM)
    kernel = functools.partial(
        exchange_kernel, n_k, len(p_blocks), len(q_blocks), n_stops, blk, tile, n_out, scale
    )
    return pl.pallas_call(
        kernel,
        out_shape=jax.ShapeDtypeStruct((n_k, n_out, 2, nb // n_out, nb), BF),
        in_specs=[pl.BlockSpec(memory_space=pltpu.SMEM)] + [vmem] * (3 + len(p_blocks) + len(q_blocks)),
        out_specs=vmem,
        scratch_shapes=[
            pltpu.VMEM((n_k, rows_p, 2 * nb), BF),
            pltpu.VMEM((n_k, rows_p, 2 * nb), BF),
            pltpu.VMEM((n_k, rows_q, 2 * nb), BF),
            pltpu.VMEM((n_k, rows_q, 2 * nb), BF),
            pltpu.VMEM((n_k, rows_p, tile), F32),
            pltpu.VMEM((n_k, rows_p, tile), F32),
            pltpu.VMEM((n_stops, rows_p, tile), F32),
            pltpu.VMEM((n_k, rows_p, 2 * tile), BF),
            pltpu.VMEM((n_k, rows_p, 2 * nb), F32),
        ],
        compiler_params=pltpu.CompilerParams(vmem_limit_bytes=60 * 1024 * 1024),
        name="block_matrices",
    )(slots, rot2, left_rows, right_rows, *p_blocks, *q_blocks)


def body(wedge_orbitals, star_members, star_ops, rotations, screen_left, screen_right):
    n_ka = lax.axis_size("ka")
    n_pt = lax.axis_size("pt")
    axes = ("ka", "pt")
    swap = functools.partial(swap_bit, axes=axes, n_ka=n_ka, n_pt=n_pt)
    me_ka = lax.axis_index("ka")
    n_wedges, mult = star_members.shape
    n_k = n_ka
    n_used = n_k - mult + 1
    _, _, p_rows, nb = wedge_orbitals.shape
    n_points = p_rows * n_pt
    n_stops, _, rank = screen_left.shape
    blk = p_rows // n_ka
    n_a = n_ka // 2
    my_a = me_ka % n_a
    my_h = me_ka // n_a

    filled = jnp.any(star_members >= 0, axis=1)
    place = jnp.cumsum(filled.astype(jnp.int32)) - 1
    wedge_iota = jnp.arange(n_wedges, dtype=jnp.int32)
    picks = (place[None, :] == jnp.arange(n_used, dtype=jnp.int32)[:, None]) & filled[None, :]
    chosen = jnp.sum(jnp.where(picks, wedge_iota[None, :], 0), axis=1)
    located = star_members[None] == jnp.arange(n_k, dtype=jnp.int32)[:, None, None]
    slots = jnp.sum(jnp.where(located, place[None, :, None], 0), axis=(1, 2)).astype(jnp.int32)
    ops = jnp.sum(jnp.where(located, star_ops[None], 0), axis=(1, 2))

    own = wedge_orbitals[:, 0].reshape(2, n_ka, blk, nb).transpose(1, 0, 2, 3)
    arrived = lax.all_to_all(own, "ka", split_axis=0, concat_axis=0, tiled=True)
    mine = jnp.stack([lax.dynamic_index_in_dim(arrived, chosen[u], 0, keepdims=False) for u in range(n_used)])

    turn = jnp.stack([lax.dynamic_index_in_dim(rotations, ops[k], 0, keepdims=False) for k in range(n_k)])
    zero = jnp.zeros_like(turn)
    rot2 = jnp.concatenate(
        [jnp.concatenate([turn, zero], axis=2), jnp.concatenate([zero, turn], axis=2)], axis=1
    )

    p_blocks = [mine]
    left_blocks = [my_a]
    bit = n_a // 2
    while bit:
        p_blocks = p_blocks + [swap(b, axis="ka", bit=bit) for b in p_blocks]
        left_blocks = left_blocks + [a ^ bit for a in left_blocks]
        bit //= 2
    left_rows = jnp.concatenate(
        [lax.dynamic_slice_in_dim(screen_left, (my_h * n_a + a) * blk, blk, 1) for a in left_blocks], axis=1
    )

    q_blocks = [mine, swap(mine, axis="ka", bit=n_a)]
    right = jnp.concatenate(
        [lax.dynamic_slice_in_dim(screen_right, ((my_h ^ h) * n_a + my_a) * blk, blk, 1) for h in (0, 1)], axis=1
    )
    bit = n_pt // 2
    while bit:
        q_blocks = q_blocks + [swap(b, axis="pt", bit=bit) for b in q_blocks]
        right = jnp.concatenate([right, swap(right, axis="pt", bit=bit)], axis=1)
        bit //= 2

    scale = 1.0 / (4.0 * n_points * math.sqrt(nb))
    partial = block_matrices(slots, rot2, left_rows, right, p_blocks, q_blocks, n_pt, scale)
    pieces = partial.reshape(n_ka * n_pt, 2, nb // n_pt, nb)
    received = lax.all_to_all(pieces, axes, split_axis=0, concat_axis=0, tiled=True)
    return jnp.sum(received.astype(F32), axis=0)[:, None]


def solution(mesh):
    return jax.shard_map(
        body,
        mesh=mesh,
        in_specs=(P(None, "ka", "pt", None), P(), P(), P(), P(None, "pt", None), P(None, "pt", None)),
        out_specs=P(None, "ka", "pt", None),
        check_vma=False,
    )
```

```python
import functools
import math

import jax
import jax.numpy as jnp
from jax import lax
from jax.experimental import pallas as pl
from jax.experimental.pallas import tpu as pltpu
from jax.sharding import PartitionSpec as P

BF = jnp.bfloat16
F32 = jnp.float32


def swap_bit(array, axes, n_ka, n_pt, axis, bit):
    route = []
    for ka in range(n_ka):
        for pt in range(n_pt):
            other = (ka ^ bit, pt) if axis == "ka" else (ka, pt ^ bit)
            route.append((ka * n_pt + pt, other[0] * n_pt + other[1]))
    return lax.ppermute(array, axes, route)


def dot_last(a, b):
    return lax.dot_general(a, b, (((1,), (1,)), ((), ())), preferred_element_type=F32)


def dot_first(a, b):
    return lax.dot_general(a, b, (((0,), (0,)), ((), ())), preferred_element_type=F32)


def read_stars(members_ref, ops_ref, slot_ref, op_ref):
    n_wedges, mult = members_ref.shape
    place = jnp.int32(0)
    for w in range(n_wedges):
        any_member = jnp.int32(0)
        for m in range(mult):
            kpoint = members_ref[w, m]

            @pl.when(kpoint >= 0)
            def _(kpoint=kpoint, place=place, w=w, m=m):
                slot_ref[kpoint] = place
                op_ref[kpoint] = ops_ref[w, m]

            any_member = jnp.where(kpoint >= 0, jnp.int32(1), any_member)
        place = place + any_member


def keep_kernel(members_ref, arrived_ref, out_ref, chosen):
    n_wedges, mult = members_ref.shape
    n_used = out_ref.shape[0]
    for u in range(n_used):
        chosen[u] = jnp.int32(0)
    place = jnp.int32(0)
    for w in range(n_wedges):
        any_member = jnp.int32(0)
        for m in range(mult):
            any_member = jnp.where(members_ref[w, m] >= 0, jnp.int32(1), any_member)

        @pl.when(any_member > 0)
        def _(place=place, w=w):
            chosen[place] = jnp.int32(w)

        place = place + any_member
    for u in range(n_used):
        out_ref[u] = arrived_ref[chosen[u]]


def keep_used(star_members, arrived, n_used):
    return pl.pallas_call(
        keep_kernel,
        out_shape=jax.ShapeDtypeStruct((n_used,) + arrived.shape[1:], arrived.dtype),
        in_specs=[pl.BlockSpec(memory_space=pltpu.SMEM), pl.BlockSpec(memory_space=pltpu.VMEM)],
        out_specs=pl.BlockSpec(memory_space=pltpu.VMEM),
        scratch_shapes=[pltpu.SMEM((n_used,), jnp.int32)],
        name="keep_used",
    )(star_members, arrived)


def plus(a, b):
    return b if a is None else a if b is None else a + b


def minus(a, b):
    if b is None:
        return a
    return -b if a is None else a - b


def scaled(a, factor):
    return None if a is None else a * factor


def direct(d, s, wrap_sign):
    n = len(d)
    out = []
    for k in range(n):
        total = None
        for i in list(range(k + 1)) + list(range(k + 1, n)):
            if s[i] is None:
                continue
            term = d[(k - i) % n] * s[i]
            total = minus(total, term) if i > k and wrap_sign < 0 else plus(total, term)
        out.append(total)
    return out


def split_factors(s):
    n = len(s)
    if n == 1 or n % 2 or all(x is None for x in s[n // 2 :]):
        return ("direct", s)
    h = n // 2
    low = [scaled(plus(s[i], s[i + h]), 0.5) for i in range(h)]
    high = [scaled(minus(s[i], s[i + h]), 0.5) for i in range(h)]
    return ("split", split_factors(low), high)


def cyclic(d, factors):
    if factors[0] == "direct":
        return direct(d, factors[1], 1)
    h = len(d) // 2
    low = cyclic([d[i] + d[i + h] for i in range(h)], factors[1])
    high = direct([d[i] - d[i + h] for i in range(h)], factors[2], -1)
    return [a + b for a, b in zip(low, high)] + [a - b for a, b in zip(low, high)]


def exchange_kernel(n_k, n_p, n_q, n_stops, blk, tile, n_out, scale, places, members_ref, star_ops_ref, where_ref,
                    rot_ref, left_ref, right_ref, *refs):
    n_right = len(places)
    got_refs = refs[:n_right]
    refs = refs[n_right:]
    p_refs = refs[:n_p]
    q_refs = refs[n_p : n_p + n_q]
    out_ref = refs[n_p + n_q]
    (slot_ref, op_ref, op, ops, oq, oql, lft, rgt, den_re0, den_im0, scr0, den_re1, den_im1, scr1, wgt0, wgt1,
     acc) = refs[n_p + n_q + 1 :]
    den_re = (den_re0, den_re1)
    den_im = (den_im0, den_im1)
    scr = (scr0, scr1)
    wgt = (wgt0, wgt1)
    rows_p = n_p * blk
    rows_q = n_q * blk
    nb = op.shape[2] // 2
    lead = n_stops // 2
    n_t = rows_q // tile
    n_it = math.gcd(n_k, rows_p // 16)
    per_it = n_k // n_it
    rows_it = rows_p // n_it

    read_stars(members_ref, star_ops_ref, slot_ref, op_ref)
    for p in range(n_p):
        lft[:, p * blk : (p + 1) * blk, :] = left_ref[:, pl.ds(pl.multiple_of(where_ref[p] * blk, blk), blk), :]
    at = 0
    for h in range(2):
        start = pl.multiple_of(where_ref[n_p + h] * blk, blk)
        rgt[:, at : at + blk, :] = right_ref[:, pl.ds(start, blk), :]
        at += blk
    for ref in got_refs:
        rgt[:, at : at + ref.shape[1], :] = ref[...]
        at += ref.shape[1]

    def rotate(k, carry):
        slot = slot_ref[k]
        parts = []
        for ref in p_refs + q_refs:
            piece = ref[slot]
            parts.append(jnp.concatenate([piece[0], piece[1]], axis=1))
        stacked = jnp.concatenate(parts, axis=0)
        turn = rot_ref[op_ref[k]]
        zero = jnp.zeros_like(turn)
        both = jnp.concatenate(
            [jnp.concatenate([turn, zero], axis=1), jnp.concatenate([zero, turn], axis=1)], axis=0
        )
        turned = jnp.dot(stacked, both, preferred_element_type=F32).astype(BF)
        first = turned[:rows_p]
        second = turned[rows_p:]
        op[k] = first
        ops[k] = jnp.concatenate([first[:, nb:], -first[:, :nb]], axis=1)
        oq[k] = second
        oql[k] = jnp.concatenate([-second[:, nb:], second[:, :nb]], axis=1)
        return carry

    lax.fori_loop(0, n_k, rotate, 0)

    def density_ops(t, i):
        cols = pl.ds(t * tile, tile)
        buf = t % 2
        jobs = []
        for jj in range(per_it):
            j = i * per_it + jj

            def real(j=j):
                den_re[buf][j] = dot_last(op[j], oq[j, cols, :])

            def imag(j=j):
                den_im[buf][j] = dot_last(ops[j], oq[j, cols, :])

            jobs += [real, imag]
        rows = pl.ds(pl.multiple_of(i * rows_it, rows_it), rows_it)

        def screens():
            for s in range(n_stops):
                scr[buf][s, rows, :] = dot_last(lft[s, rows, :], rgt[s, cols, :])

        return jobs + [screens]

    def weigh_ops(t, i):
        buf = t % 2
        jobs = []
        for strip in range(rows_it // 16):
            for chunk in range(tile // 128):

                def weigh(strip=strip, chunk=chunk):
                    first = pl.multiple_of(i * rows_it + strip * 16, 16)
                    lanes = pl.ds(chunk * 128, 128)
                    halves = []
                    for r in range(2):
                        rows = pl.ds(pl.multiple_of(first + r * 8, 8), 8)
                        screens = [scr[buf][s, rows, lanes] for s in range(n_stops)]
                        factors = split_factors(screens + [None] * (n_k - n_stops))
                        outs = []
                        for den in (den_re[buf], den_im[buf]):
                            d = [den[(j + lead) % n_k, rows, lanes] for j in range(n_k)]
                            outs.append(cyclic(d, factors))
                        halves.append(outs)
                    for part in range(2):
                        for k in range(n_k):
                            both = jnp.concatenate([halves[0][part][k], halves[1][part][k]], axis=0)
                            wgt[buf][k, pl.ds(first, 16), pl.ds(part * tile + chunk * 128, 128)] = both.astype(BF)

                jobs.append(weigh)
        return jobs

    def apply_ops(t, i):
        cols = pl.ds(t * tile, tile)
        buf = t % 2
        jobs = []
        for kk in range(per_it):
            k = i * per_it + kk

            def apply(k=k):
                weights = jnp.concatenate([oq[k, cols, :], oql[k, cols, :]], axis=0)
                product = jnp.dot(wgt[buf][k], weights, preferred_element_type=F32)
                acc[k] = product if t == 0 else acc[k] + product

            jobs.append(apply)
        return jobs

    for stage in range(n_t + 2):

        def step(i, carry, stage=stage):
            matrix = []
            vector = []
            if stage < n_t:
                matrix += density_ops(stage, i)
            if 0 <= stage - 2:
                matrix += apply_ops(stage - 2, i)
            if 0 <= stage - 1 < n_t:
                vector += weigh_ops(stage - 1, i)
            n_m, n_v = len(matrix), len(vector)
            done = 0
            for m, job in enumerate(matrix):
                job()
                upto = (m + 1) * n_v // n_m
                for v in range(done, upto):
                    vector[v]()
                done = upto
            for v in range(done, n_v):
                vector[v]()
            return carry

        lax.fori_loop(0, n_it, step, 0)

    def project(k, carry):
        gram = dot_first(op[k], acc[k].astype(BF)) * scale
        real = (gram[:nb, :nb] + gram[nb:, nb:]).astype(BF)
        imag = (gram[:nb, nb:] - gram[nb:, :nb]).astype(BF)
        step = nb // n_out
        for o in range(n_out):
            out_ref[k, o, 0] = real[o * step : (o + 1) * step]
            out_ref[k, o, 1] = imag[o * step : (o + 1) * step]
        return carry

    lax.fori_loop(0, n_k, project, 0)


def block_matrices(stars, star_ops, where, rotations, left, right, got, p_blocks, q_blocks, n_k, n_out, scale):
    blk, nb = p_blocks[0].shape[2:]
    n_stops, _, rank = left.shape
    rows_p = len(p_blocks) * blk
    rows_q = len(q_blocks) * blk
    tile = min(256, rows_q)
    vmem = pl.BlockSpec(memory_space=pltpu.VMEM)
    smem = pl.BlockSpec(memory_space=pltpu.SMEM)
    places = tuple(g.shape[1] for g in got)
    kernel = functools.partial(
        exchange_kernel, n_k, len(p_blocks), len(q_blocks), n_stops, blk, tile, n_out, scale, places
    )
    tiles = [
        pltpu.VMEM((n_k, rows_p, tile), F32),
        pltpu.VMEM((n_k, rows_p, tile), F32),
        pltpu.VMEM((n_stops, rows_p, tile), F32),
    ]
    return pl.pallas_call(
        kernel,
        out_shape=jax.ShapeDtypeStruct((n_k, n_out, 2, nb // n_out, nb), BF),
        in_specs=[smem] * 3 + [vmem] * (3 + len(got) + len(p_blocks) + len(q_blocks)),
        out_specs=vmem,
        scratch_shapes=[
            pltpu.SMEM((n_k,), jnp.int32),
            pltpu.SMEM((n_k,), jnp.int32),
            pltpu.VMEM((n_k, rows_p, 2 * nb), BF),
            pltpu.VMEM((n_k, rows_p, 2 * nb), BF),
            pltpu.VMEM((n_k, rows_q, 2 * nb), BF),
            pltpu.VMEM((n_k, rows_q, 2 * nb), BF),
            pltpu.VMEM((n_stops, rows_p, rank), BF),
            pltpu.VMEM((n_stops, rows_q, rank), BF),
        ]
        + tiles
        + tiles
        + [
            pltpu.VMEM((n_k, rows_p, 2 * tile), BF),
            pltpu.VMEM((n_k, rows_p, 2 * tile), BF),
            pltpu.VMEM((n_k, rows_p, 2 * nb), F32),
        ],
        compiler_params=pltpu.CompilerParams(vmem_limit_bytes=60 * 1024 * 1024),
        name="block_matrices",
    )(stars, star_ops, where, rotations, left, right, *got, *p_blocks, *q_blocks)


def body(wedge_orbitals, star_members, star_ops, rotations, screen_left, screen_right):
    n_ka = lax.axis_size("ka")
    n_pt = lax.axis_size("pt")
    axes = ("ka", "pt")
    swap = functools.partial(swap_bit, axes=axes, n_ka=n_ka, n_pt=n_pt)
    me_ka = lax.axis_index("ka")
    mult = star_members.shape[1]
    n_k = n_ka
    n_used = n_k - mult + 1
    _, _, p_rows, nb = wedge_orbitals.shape
    n_points = p_rows * n_pt
    blk = p_rows // n_ka
    n_a = n_ka // 2
    my_a = me_ka % n_a
    my_h = me_ka // n_a

    own = wedge_orbitals[:, 0].reshape(2, n_ka, blk, nb).transpose(1, 0, 2, 3)
    arrived = lax.all_to_all(own, "ka", split_axis=0, concat_axis=0, tiled=True)
    mine = keep_used(star_members, arrived, n_used)

    p_blocks = [mine]
    places = [my_a]
    bit = n_a // 2
    while bit:
        p_blocks = p_blocks + [swap(b, axis="ka", bit=bit) for b in p_blocks]
        places = places + [a ^ bit for a in places]
        bit //= 2
    where = jnp.stack([my_h * n_a + a for a in places] + [(my_h ^ h) * n_a + my_a for h in (0, 1)]).astype(jnp.int32)

    q_blocks = [mine, swap(mine, axis="ka", bit=n_a)]
    right = jnp.concatenate(
        [lax.dynamic_slice_in_dim(screen_right, ((my_h ^ h) * n_a + my_a) * blk, blk, 1) for h in (0, 1)], axis=1
    )
    got = []
    bit = n_pt // 2
    while bit:
        q_blocks = q_blocks + [swap(b, axis="pt", bit=bit) for b in q_blocks]
        got = got + [swap(b, axis="pt", bit=bit) for b in [right] + got]
        bit //= 2

    scale = 1.0 / (4.0 * n_points * math.sqrt(nb))
    partial = block_matrices(
        star_members, star_ops, where, rotations, screen_left, screen_right, got, p_blocks, q_blocks, n_k, n_pt, scale
    )
    pieces = partial.reshape(n_ka * n_pt, 2, nb // n_pt, nb)
    received = lax.all_to_all(pieces, axes, split_axis=0, concat_axis=0, tiled=True)
    return jnp.sum(received.astype(F32), axis=0)[:, None]


def solution(mesh):
    return jax.shard_map(
        body,
        mesh=mesh,
        in_specs=(P(None, "ka", "pt", None), P(), P(), P(), P(None, "pt", None), P(None, "pt", None)),
        out_specs=P(None, "ka", "pt", None),
        check_vma=False,
    )
```
